256 devices in a mesh: pair: 32 (over y, z), aux: 8 (over x, core).
Axes of the slice: x: 4, y: 4, z: 8, core: 2. Of those that a mesh axis runs over, the one named last changes fastest.
Arguments:
- three_center: bfloat16 [8192, 32, 2048], P(('pair', 'aux')), may hold values from -1 to 1
- panel: bfloat16 [512, 64], P('pair'), may hold values from -6 to 6
- metric: float32 [256, 64, 64], P(('pair', 'aux')), may hold values from -0.5 to 1.6
- screen: int32 [32, 256, 1], P(None, 'aux'), may hold values from 0 to 31; in each aligned block of 32 rows (0 to 31, 32 to 63, ..., all dimensions but the last counted through in order) at most 2 rows name the same one
- pair_blocks: int32 [32, 256, 2], P(None, 'aux'), may hold values from 0 to 15
Outputs:
- fitted: bfloat16 [256, 512, 4096], P(('pair', 'aux'))
- exchange: float32 [512, 512], P(('pair', 'aux'))
The draws below stay inside these ranges and needn't reach their ends.
Inputs may be any that keep to these rules, and one draw needn't show every extreme that they name: `screen`: in the list of one device no pair index is named by more than 2 slots, and in some lists one is named exactly 2 times.
All inputs are finite; a program needn't handle non-finite values.
Results may differ from the reference program's by a relative error of at most 0.0049.
Values may be sent and summed in bfloat16 or wider, within the bound.
No kernel may reach another device: no remote copies, remote signals or barrier semaphores. Data moves between devices by JAX's collectives and lax.ppermute only.
A program may use at most 192 MiB of HBM per device.

```python
import math
import jax
import jax.numpy as jnp
import numpy as np
from jax import lax

FB = 32
NBLK = 16
AB = 64
OCC = 64
SLOTS = 32
CAP = 2
NBF = 512
NQ = 256
N_PAIR = 32
N_AUX = 8


def draw_metric(key, part):
    first_key, second_key = jax.random.split(key)
    indices = jnp.arange(AB)
    diagonal_mask = indices[:, None] == indices[None, :]
    offdiag = jax.random.normal(first_key, (NQ, AB, AB), jnp.float32) * (0.5 / math.sqrt(AB))
    diagonal = jax.random.uniform(second_key, (NQ, AB, AB), jnp.float32, 0.8, 1.2)
    offdiag = jnp.clip(offdiag, -0.5, 0.5)
    return jnp.where(diagonal_mask[None, :, :], diagonal, offdiag)


def touch_ends(array, key, smallest, high):
    spot = [jax.random.randint(jax.random.fold_in(key, axis), (), 0, length) for axis, length in enumerate(array.shape)]
    widest = array.shape.index(max(array.shape))
    next_to = spot[:widest] + [(spot[widest] + 1) % array.shape[widest]] + spot[widest + 1:]
    return array.at[tuple(spot)].set(smallest).at[tuple(next_to)].set(high)


def levels(stream_key, dims, pieces, least, largest):
    level = 1.0
    for axis_at, blocks in pieces:
        draws = jax.random.uniform(jax.random.fold_in(jax.random.fold_in(stream_key, 6), axis_at), (blocks,), jnp.float32, least / len(pieces), largest / len(pieces))
        level = level * jnp.repeat(jnp.exp(draws), dims[axis_at] // blocks).reshape((-1,) + (1,) * (len(dims) - 1 - axis_at))
    return level


def shared_out(rng, own, number, rows, number_of, top, most, skew):
    sequence = jax.random.permutation(rng, number_of)
    crowded, ordinary = portions_of(number_of, rows * top, most, skew, True), portions_of(number_of, rows * top, most, skew, False)
    places = jnp.arange(number_of)

    def named(lengths, offset_by):
        used = int((lengths > 0).sum())
        fixed = max(1, used // 4)
        moved = fixed + (places - fixed + offset_by * (used - fixed)) % max(1, number_of - fixed)
        return jnp.zeros((number_of,), jnp.int32).at[sequence[jnp.where(places < fixed, places, moved)]].set(jnp.asarray(lengths, jnp.int32))

    lengths = jnp.where(number % 4 == 0, named(crowded, number // 4), named(ordinary, number - number // 4 - 1))
    mixed = jax.random.permutation(jax.random.fold_in(own, 3), number_of)
    donor, receiver = mixed[0:number_of // 2 * 2:2], mixed[1:number_of // 2 * 2:2]
    room = jnp.minimum(lengths[donor] - 1, most - lengths[receiver]) // 2
    room = jnp.where((donor == sequence[0]) | (receiver == sequence[0]) | (lengths[receiver] == 0), 0, jnp.maximum(room, 0))
    moved = jax.random.randint(jax.random.fold_in(own, 4), (number_of // 2,), 0, 1 << 20) % (room + 1)
    lengths = lengths.at[donor].add(-moved).at[receiver].add(moved)
    members = jnp.searchsorted(jnp.cumsum(lengths), jnp.arange(rows * top), side="right").astype(jnp.int32)
    grid = members.reshape(top, rows).T
    grid = grid[jax.random.permutation(jax.random.fold_in(own, 1), rows)]
    offset_by = jax.random.randint(jax.random.fold_in(own, 2), (rows, 1), 0, top)
    return jnp.take_along_axis(grid, (jnp.arange(top)[None, :] + offset_by) % top, axis=1)


def portions_of(amount, total, bound, slope, full):
    portions = [(1 << 20) // math.isqrt(grade ** slope) + 1 for grade in range(1, amount + 1)]
    largest = bound if full else min(bound, max(-(-total // amount), total * portions[0] // sum(portions)))
    least = 1 if total - largest >= amount - 1 else 0
    holding, surplus = [largest] + [least] * (amount - 1), total - largest - least * (amount - 1)
    while surplus > 0:
        free = [i for i in range(1, amount) if holding[i] < largest] or [i for i in range(1, amount) if holding[i] < bound]
        mass, left = sum([portions[i] for i in free]), surplus
        for i in free:
            extra = min(bound - holding[i], max(1, left * portions[i] // mass), surplus)
            holding[i] = holding[i] + extra
            surplus = surplus - extra
    return np.array(holding)


def noise(stream_key, extent, scale, limit, cuts=(), held_as=jnp.bfloat16):
    array = jax.random.normal(stream_key, extent, jnp.float32) * scale
    if len(cuts) > 0:
        array = levels(stream_key, extent, cuts, -0.22, 0.18) * array
    return jnp.clip(array, min=-limit, max=limit).astype(held_as)


def setup_inputs(seed: int = 0) -> dict:
    key_of = jax.random.split(jax.random.key(seed), 6)
    three_center = noise(key_of[0], (N_PAIR * N_AUX * SLOTS, FB, AB * FB), FB ** -0.5, 1.0, ((0, 256),))
    panel = noise(key_of[1], (NBF, OCC), 1.0, 6.0, ((0, 32),))
    metric = draw_metric(jax.random.fold_in(key_of[5], 71), 0)
    screen_keys = jax.random.split(jax.random.fold_in(key_of[3], 1), N_PAIR * (N_AUX * SLOTS) // SLOTS)
    screen_turns = jax.random.permutation(jax.random.fold_in(key_of[3], 3), N_PAIR * (N_AUX * SLOTS) // SLOTS)
    screen = jax.vmap(lambda own, number: shared_out(jax.random.fold_in(key_of[3], 2), own, number, SLOTS, N_PAIR, 1, CAP, 2))(screen_keys, screen_turns).reshape((N_PAIR, N_AUX * SLOTS, 1))
    pair_blocks = touch_ends(jax.random.randint(key_of[4], (N_PAIR, N_AUX * SLOTS, 2), 0, NBLK), jax.random.fold_in(key_of[4], 1), 0, NBLK - 1).astype(jnp.int32)
    return {"three_center": three_center, "panel": panel, "metric": metric, "screen": screen, "pair_blocks": pair_blocks}


def reference(three_center, panel, metric, screen, pair_blocks):
    basis_total = NBLK * FB
    integrals = three_center.reshape(N_PAIR, N_AUX, SLOTS, FB, AB, FB)
    integrals = jnp.moveaxis(integrals, 1, 0).reshape(N_AUX, N_PAIR * SLOTS, FB, AB, FB)
    targets = jnp.moveaxis(screen.reshape(N_PAIR, N_AUX, SLOTS), 1, 0).reshape(N_AUX, N_PAIR * SLOTS)
    block_ids = jnp.moveaxis(pair_blocks.reshape(N_PAIR, N_AUX, SLOTS, 2), 1, 0).reshape(N_AUX, N_PAIR * SLOTS, 2)
    factors = jnp.moveaxis(metric.reshape(N_PAIR, N_AUX, AB, AB), 1, 0)
    panel_blocks = panel.astype(jnp.float32).reshape(NBLK, FB, OCC)

    def column(accumulated, inputs):
        column_ints, column_targets, column_blocks, column_factors = inputs
        picked = panel_blocks[column_blocks[:, 1]]
        transformed = jnp.einsum('smqn,sni->smqi', column_ints.astype(jnp.float32), picked)
        transformed = lax.optimization_barrier(transformed.astype(jnp.bfloat16)).astype(jnp.float32)
        segment_ids = (column_targets * NBLK + column_blocks[:, 0]).astype(jnp.int32)
        summed = jax.ops.segment_sum(transformed, segment_ids, num_segments=N_PAIR * NBLK)
        summed = summed.reshape(N_PAIR, basis_total, AB, OCC)
        fitted = jnp.einsum('dpq,drqi->drpi', column_factors, summed, precision=lax.Precision.HIGHEST)
        fitted = fitted.astype(jnp.bfloat16).reshape(N_PAIR, basis_total, AB * OCC)
        widened = fitted.astype(jnp.float32)
        column_sum = jnp.einsum('drx,dcx->rc', widened, widened)
        return accumulated + column_sum, fitted

    start_value = jnp.zeros((basis_total, basis_total), jnp.float32)
    accumulated, fitted_all = lax.scan(column, start_value, (integrals, targets, block_ids, factors))
    fitted_all = jnp.moveaxis(fitted_all, 0, 1).reshape(N_PAIR * N_AUX, basis_total, AB * OCC)
    norm_factor = 1.0 / (N_PAIR * N_AUX * AB * OCC)
    return fitted_all, accumulated * norm_factor
```

```python
import functools
import jax
import jax.numpy as jnp
from jax import lax
from jax.experimental import pallas as pl
from jax.experimental.pallas import tpu as pltpu
from jax.sharding import PartitionSpec as P

BF = jnp.bfloat16
F32 = jnp.float32


def iota(shape, dim):
    return lax.broadcasted_iota(jnp.int32, shape, dim)


def ones_where(mask):
    return jnp.where(mask, 1.0, 0.0).astype(BF)


def nt_dot(a, b):
    return lax.dot_general(a, b, (((1,), (1,)), ((), ())), preferred_element_type=F32)


def nn_dot(a, b):
    return jnp.dot(a, b, preferred_element_type=F32)


def pack_kernel(slots, position, blocks, out, held, in_sem, out_sem):
    def fetch(s):
        return pltpu.make_async_copy(blocks.at[s], held.at[s], in_sem.at[s])

    def put(s):
        return pltpu.make_async_copy(held.at[s], out.at[position[s]], out_sem.at[s])

    @pl.loop(0, slots)
    def _(s):
        fetch(s).start()

    @pl.loop(0, slots)
    def _(s):
        fetch(s).wait()
        put(s).start()

    @pl.loop(0, slots)
    def _(s):
        put(s).wait()


def pack(position, blocks, rows):
    slots, width, inner = blocks.shape
    return pl.pallas_call(
        functools.partial(pack_kernel, slots),
        out_shape=jax.ShapeDtypeStruct((rows, width, inner), blocks.dtype),
        grid_spec=pltpu.PrefetchScalarGridSpec(
            num_scalar_prefetch=1,
            grid=(1,),
            in_specs=[pl.BlockSpec(memory_space=pl.ANY)],
            out_specs=pl.BlockSpec(memory_space=pl.ANY),
            scratch_shapes=[
                pltpu.VMEM((slots, width, inner), blocks.dtype),
                pltpu.SemaphoreType.DMA((slots,)),
                pltpu.SemaphoreType.DMA((slots,)),
            ],
        ),
        name="pack",
    )(position, blocks)


def swap_groups(parts, lane_group):
    for step in (4, 2, 1):
        low = (lane_group & step) == 0
        done = list(parts)
        for j in range(8):
            if j & step:
                continue
            a, b = parts[j], parts[j + step]
            done[j] = jnp.where(low, a, pltpu.roll(b, 16 * step, 1))
            done[j + step] = jnp.where(low, pltpu.roll(a, 128 - 16 * step, 1), b)
        parts = done
    return parts


def owner_kernel(
    sizes, valid, mu_of, nu_of, blocks, panel, metric, row_of, fitted_out, partial_out,
    held, acc, weights, xs, ys, fitted, in_sem, out_sem,
):
    rows, nbasis, fb, ab, occ, rb = sizes
    nblk = nbasis // fb
    tiles = ab // 4
    wide = ab * occ

    def fetch(j):
        return pltpu.make_async_copy(blocks.at[j], held.at[j], in_sem.at[j])

    @pl.loop(0, rows)
    def _(j):
        @pl.when(valid[j] > 0)
        def _():
            fetch(j).start()

    @pl.loop(0, nbasis // 8)
    def _(r):
        acc[pl.ds(pl.multiple_of(r * 8, 8), 8), :] = jnp.zeros((8, wide), F32)

    spread_row = iota((occ, 256), 0)
    spread_col = iota((occ, 256), 1)
    spread = ones_where((spread_col // 16) * 4 + spread_col % 4 == spread_row)
    same_q = iota((4 * fb, 256), 0) // fb == (iota((4 * fb, 256), 1) // 4) % 4

    @pl.loop(0, nblk)
    def _(n):
        part = panel[pl.ds(pl.multiple_of(n * fb, fb), fb), :]
        stacked = jnp.concatenate([part] * 4, axis=0)
        weights[n] = jnp.where(same_q, nn_dot(stacked, spread), 0.0).astype(BF)

    @pl.loop(0, rows)
    def _(j):
        @pl.when(valid[j] > 0)
        def _():
            fetch(j).wait()
            block = held[j]
            lhs = jnp.concatenate(
                [block[:, c * 128 : (c + 1) * 128] for c in range(tiles)], axis=0
            )
            half = nn_dot(lhs, weights[nu_of[j]]).astype(BF).astype(F32)
            at = pl.ds(pl.multiple_of(mu_of[j] * fb, fb), fb)
            for c in range(tiles):
                acc[at, c * 256 : (c + 1) * 256] += half[c * fb : (c + 1) * fb, :]

    expand = ones_where(iota((256, ab), 0) // 4 == iota((256, ab), 1))
    same_i = iota((256, 256), 0) % 4 == iota((256, 256), 1) % 4
    whole = metric[...]
    high = whole.astype(BF)
    low = (whole - high.astype(F32)).astype(BF)

    def widen(part):
        tall = nt_dot(expand, part).astype(BF)
        return jnp.where(same_i, nt_dot(tall, expand), 0.0).astype(BF)

    metric_high = widen(high)
    metric_low = widen(low)
    lane_from = iota((256, 256), 0)
    lane_to = iota((256, 256), 1)
    order = ones_where(
        ((lane_from // 4) % 4) * 64 + (lane_from // 16) * 4 + lane_from % 4 == lane_to
    )
    lane_group = iota((rb, 128), 1) // 16

    @pl.loop(0, nbasis // rb)
    def _(step):
        base = pl.multiple_of(step * rb, rb)
        at = pl.ds(base, rb)
        for ch in range(2):
            for h in range(2):
                parts = [
                    acc[at, (8 * ch + j) * 256 + h * 128 : (8 * ch + j) * 256 + h * 128 + 128]
                    for j in range(8)
                ]
                parts = swap_groups(parts, lane_group)
                for g in range(8):
                    xs[(8 * h + g) * rb : (8 * h + g + 1) * rb, ch * 128 : ch * 128 + 128] = parts[g]
        x = xs[...]
        x_high = x.astype(BF)
        x_low = (x - x_high.astype(F32)).astype(BF)
        y = nn_dot(x_high, metric_high) + nn_dot(x_low, metric_high) + nn_dot(x_high, metric_low)
        ys[...] = y.astype(BF).astype(F32)
        for ch in range(2):
            for h in range(2):
                parts = [
                    ys[(8 * ch + j) * rb : (8 * ch + j + 1) * rb, h * 128 : h * 128 + 128]
                    for j in range(8)
                ]
                parts = swap_groups(parts, lane_group)
                for g in range(8):
                    xs[(8 * h + g) * rb : (8 * h + g + 1) * rb, ch * 128 : ch * 128 + 128] = parts[g]
        f = nn_dot(xs[...].astype(BF), order).astype(BF)
        for c in range(tiles):
            fitted[at, c * 256 : (c + 1) * 256] = f[c * rb : (c + 1) * rb, :]
        pltpu.make_async_copy(fitted.at[at, :], fitted_out.at[at, :], out_sem.at[step]).start()

    total = jnp.zeros((nbasis, nbasis), F32)
    for k in range(wide // 512):
        part = fitted[:, k * 512 : (k + 1) * 512]
        total = total + nt_dot(part, part)
    pick = ones_where(row_of[...] == iota((nbasis, nbasis), 1))
    partial_out[...] = nn_dot(pick, total.astype(BF)).astype(BF)

    @pl.loop(0, nbasis // rb)
    def _(step):
        at = pl.ds(pl.multiple_of(step * rb, rb), rb)
        pltpu.make_async_copy(fitted.at[at, :], fitted_out.at[at, :], out_sem.at[step]).wait()


def owner(valid, mu_of, nu_of, blocks, panel, metric, row_of):
    rows, fb, inner = blocks.shape
    nbasis, occ = panel.shape
    ab = metric.shape[0]
    rb = 32
    wide = ab * occ
    vmem = pl.BlockSpec(memory_space=pltpu.VMEM)
    anywhere = pl.BlockSpec(memory_space=pl.ANY)
    return pl.pallas_call(
        functools.partial(owner_kernel, (rows, nbasis, fb, ab, occ, rb)),
        out_shape=(
            jax.ShapeDtypeStruct((nbasis, wide), BF),
            jax.ShapeDtypeStruct((nbasis, nbasis), BF),
        ),
        grid_spec=pltpu.PrefetchScalarGridSpec(
            num_scalar_prefetch=3,
            grid=(1,),
            in_specs=[anywhere, vmem, vmem, vmem],
            out_specs=(anywhere, vmem),
            scratch_shapes=[
                pltpu.VMEM((rows, fb, inner), BF),
                pltpu.VMEM((nbasis, wide), F32),
                pltpu.VMEM((nbasis // fb, 4 * fb, 256), BF),
                pltpu.VMEM((16 * rb, 256), F32),
                pltpu.VMEM((16 * rb, 256), F32),
                pltpu.VMEM((nbasis, wide), BF),
                pltpu.SemaphoreType.DMA((rows,)),
                pltpu.SemaphoreType.DMA((nbasis // rb,)),
            ],
        ),
        compiler_params=pltpu.CompilerParams(vmem_limit_bytes=48 << 20),
        name="owner",
    )(valid, mu_of, nu_of, blocks, panel, metric, row_of)


def shards(three_center, panel, metric, screen, pair_blocks):
    pair_count = lax.axis_size("pair")
    column_count = lax.axis_size("aux")
    own = lax.axis_index("pair")
    slots, fb, inner = three_center.shape
    ab = metric.shape[1]
    occ = panel.shape[1]
    nbasis = panel.shape[0] * pair_count
    capacity = 2
    targets = screen[:, :, 0]
    ids = jnp.arange(slots)
    earlier = ids[None, :] < ids[:, None]
    own_targets = lax.dynamic_index_in_dim(targets, own, 0, keepdims=False)
    own_ranks = jnp.sum(((own_targets[:, None] == own_targets[None, :]) & earlier).astype(jnp.int32), axis=1)
    position = own_targets * capacity + own_ranks
    outgoing = pack(position, three_center, pair_count * capacity)
    outgoing = outgoing.reshape(pair_count, capacity, fb, inner)

    whole_panel = lax.all_to_all(
        jnp.broadcast_to(panel[None], (pair_count,) + panel.shape), "pair", 0, 0, tiled=True
    ).reshape(nbasis, occ)
    arrived = lax.all_to_all(outgoing, "pair", 0, 0, tiled=True)

    mine = targets == own
    before = jnp.cumsum(mine.astype(jnp.int32), axis=1) - mine.astype(jnp.int32)
    hits = mine[:, None, :] & (before[:, None, :] == jnp.arange(capacity)[None, :, None])
    flat = pair_count * capacity
    valid = jnp.sum(hits.astype(jnp.int32), axis=2).reshape(flat)
    mu_of = jnp.sum(jnp.where(hits, pair_blocks[:, None, :, 0], 0), axis=2).reshape(flat)
    nu_of = jnp.sum(jnp.where(hits, pair_blocks[:, None, :, 1], 0), axis=2).reshape(flat)

    share = nbasis // (pair_count * column_count)
    row_of = jnp.arange(nbasis).reshape(pair_count, column_count, share)
    row_of = row_of.transpose(1, 0, 2).reshape(nbasis, 1)
    fitted, partial = owner(
        valid, mu_of, nu_of, arrived.reshape(flat, fb, inner), whole_panel, metric[0], row_of
    )
    partial = lax.all_to_all(
        partial.reshape(column_count, nbasis // column_count, nbasis), "aux", 0, 0, tiled=True
    )
    partial = jnp.sum(partial.astype(F32), axis=0).reshape(pair_count, share, nbasis)
    partial = lax.all_to_all(partial, "pair", 0, 0, tiled=True)
    norm_factor = 1.0 / (pair_count * column_count * ab * occ)
    return (fitted[None], jnp.sum(partial, axis=0) * norm_factor)


def solution(mesh):
    return jax.shard_map(
        shards,
        mesh=mesh,
        in_specs=(
            P(("pair", "aux"), None, None),
            P("pair", None),
            P(("pair", "aux"), None, None),
            P(None, "aux", None),
            P(None, "aux", None),
        ),
        out_specs=(P(("pair", "aux"), None, None), P(("pair", "aux"), None)),
        check_vma=False,
    )
```

```python
import functools
import jax
import jax.numpy as jnp
from jax import lax
from jax.experimental import pallas as pl
from jax.experimental.pallas import tpu as pltpu
from jax.sharding import PartitionSpec as P

BF = jnp.bfloat16
F32 = jnp.float32
SUBS = 4
YT = jnp.float32


def iota(shape, dim):
    return lax.broadcasted_iota(jnp.int32, shape, dim)


def ones_where(mask):
    return jnp.where(mask, 1.0, 0.0).astype(BF)


def nt_dot(a, b):
    return lax.dot_general(a, b, (((1,), (1,)), ((), ())), preferred_element_type=F32)


def nn_dot(a, b):
    return jnp.dot(a, b, preferred_element_type=F32)


def pack_kernel(slots, planes, crowd, target, second, order, blocks, out_a, out_b, out_c, out_d, held, in_sem, out_sem):
    width = held.shape[2]
    half, quarter = width // 2, width // 4
    rows = out_a.shape[0] // planes

    def fetch(s):
        return pltpu.make_async_copy(blocks.at[s], held.at[s], in_sem.at[s])

    def put(s, part, lane, size, to):
        return pltpu.make_async_copy(held.at[s, :, pl.ds(lane, size)], to, out_sem.at[s, part])

    def puts(s, act):
        t = target[s]

        @pl.when((second[s] == 0) & (crowd[0] != 2))
        def _():
            act(put(s, 0, 0, half, out_a.at[t, :, pl.ds(0, half)]))
            act(put(s, 1, half, half, out_b.at[t]))

        @pl.when((second[s] == 0) & (crowd[0] == 2))
        def _():
            act(put(s, 0, 0, quarter, out_a.at[t, :, pl.ds(0, quarter)]))
            act(put(s, 1, quarter, width - quarter, out_c.at[t]))

        for y in range(rows):
            peer = y * planes + lax.rem(t, planes)

            @pl.when((second[s] > 0) & (crowd[0] <= 1))
            def _():
                act(put(s, y, y * quarter, quarter, out_a.at[peer, :, pl.ds(half, quarter)]))

            @pl.when((second[s] > 0) & (crowd[0] == 2))
            def _():
                lane = pl.multiple_of(quarter + order[s] * quarter, quarter)
                act(put(s, y, y * quarter, quarter, out_a.at[peer, :, pl.ds(lane, quarter)]))

        @pl.when((second[s] > 0) & (crowd[0] > 2))
        def _():
            act(put(s, 0, 0, width, out_d.at[t]))

    @pl.loop(0, slots)
    def _(s):
        fetch(s).start()

    @pl.loop(0, slots)
    def _(s):
        fetch(s).wait()
        puts(s, lambda copy: copy.start())

    @pl.loop(0, slots)
    def _(s):
        puts(s, lambda copy: copy.wait())


def pack(crowd, target, second, order, blocks, owners, planes):
    slots, fb, inner = blocks.shape
    anywhere = pl.BlockSpec(memory_space=pl.ANY)
    shape = lambda lanes: jax.ShapeDtypeStruct((owners, fb, lanes), blocks.dtype)
    return pl.pallas_call(
        functools.partial(pack_kernel, slots, planes),
        out_shape=(shape(inner // 4 * 3), shape(inner // 2), shape(inner // 4 * 3), shape(inner)),
        grid_spec=pltpu.PrefetchScalarGridSpec(
            num_scalar_prefetch=4,
            grid=(1,),
            in_specs=[anywhere],
            out_specs=(anywhere,) * 4,
            scratch_shapes=[
                pltpu.VMEM((slots, fb, inner), blocks.dtype),
                pltpu.SemaphoreType.DMA((slots,)),
                pltpu.SemaphoreType.DMA((slots, 4)),
            ],
        ),
        compiler_params=pltpu.CompilerParams(vmem_limit_bytes=60 << 20),
        name="pack",
    )(crowd, target, second, order, blocks)


def swap_groups(parts):
    count = len(parts)
    group = 128 // count
    lane_group = iota(parts[0].shape, 1) // group
    step = count // 2
    while step:
        low = (lane_group & step) == 0
        done = list(parts)
        for j in range(count):
            if j & step:
                continue
            a, b = parts[j], parts[j + step]
            done[j] = jnp.where(low, a, pltpu.roll(b, group * step, 1))
            done[j + step] = jnp.where(low, pltpu.roll(a, 128 - group * step, 1), b)
        parts = done
        step //= 2
    return parts


def pieces(kind, row, rows, places, inner, p, second, order):
    half, quarter = inner // 2, inner // 4
    if not second:
        split = quarter if kind == 2 else half
        return [(0, p, 0, 0, split, None), (1, p, 0, split, inner - split, None)]
    if kind == 3:
        return [(2, p, 0, 0, inner, None)]
    first = half if kind == 1 else quarter
    shift = 0 if kind == 1 else order * quarter
    at = lambda y: pl.multiple_of(lax.rem(row + y, rows) * quarter, quarter)
    low = p < places // 2
    return [
        (0, p, first + shift, at(0), quarter, None),
        (2, p, shift, at(rows - 1), quarter, None),
        (3, p, shift, at(1), quarter, None),
        (4, p, shift, at(2), quarter, low),
        (5, p - places // 2, shift, at(2), quarter, jnp.logical_not(low)),
    ]


def owner_kernel(
    kind, count, sizes, valid, mu_of, nu_of, order_of, row, *refs
):
    blocks = refs[:count]
    (panel, metric, row_of, fitted_out, partial_out, held, acc, weights, xs_all, ys_all, zs_all,
     total, fitted, in_sem, out_sem) = refs[count:]
    owner_body(kind, blocks, sizes, valid, mu_of, nu_of, order_of, row, panel, metric, row_of, fitted_out,
               partial_out, held, acc, weights, xs_all, ys_all, zs_all, total, fitted, in_sem, out_sem)


def owner_body(
    kind, blocks, sizes, valid, mu_of, nu_of, order_of, row, panel, metric, row_of, fitted_out, partial_out,
    held, acc, weights, xs_all, ys_all, zs_all, total, fitted, in_sem, out_sem,
):
    rows, nbasis, fb, ab, occ, rb, plane_rows = sizes
    places = rows // 2
    inner = ab * fb
    nblk = nbasis // fb
    tiles = ab // 4
    wide = ab * occ

    def fetch(j, p, second, act):
        found = pieces(kind, row[0], plane_rows, places, inner, p, second, order_of[p])
        for k, (source, index, lane, to, size, when) in enumerate(found):
            def go():
                act(pltpu.make_async_copy(
                    blocks[source].at[index, :, pl.ds(pl.multiple_of(lane, 128), size)],
                    held.at[j, :, pl.ds(to, size)],
                    in_sem.at[j, k],
                ))
            if when is None:
                go()
            else:
                pl.when(when)(go)

    for second in range(2):
        @pl.loop(0, places)
        def _(p):
            j = second * places + p

            @pl.when(valid[j] > 0)
            def _():
                fetch(j, p, second, lambda copy: copy.start())

    @pl.loop(0, nbasis // 8)
    def _(r):
        acc[pl.ds(pl.multiple_of(r * 8, 8), 8), :] = jnp.zeros((8, wide), F32)

    spread_row = iota((occ, 512), 0)
    spread_col = iota((occ, 512), 1)
    spread = ones_where((spread_col // 32) * 4 + spread_col % 4 == spread_row)
    same_q = iota((8 * fb, 512), 0) // fb == (iota((8 * fb, 512), 1) // 4) % 8

    @pl.loop(0, nblk)
    def _(n):
        part = panel[pl.ds(pl.multiple_of(n * fb, fb), fb), :]
        stacked = jnp.concatenate([part] * 8, axis=0)
        weights[n] = jnp.where(same_q, nn_dot(stacked, spread), 0.0).astype(BF)

    def add_block(j):
        block = held[j]
        lhs = jnp.concatenate(
            [block[:, c * 256 : (c + 1) * 256] for c in range(tiles // 2)], axis=0
        )
        half = nn_dot(lhs, weights[nu_of[j]]).astype(BF).astype(F32)
        at = pl.ds(pl.multiple_of(mu_of[j] * fb, fb), fb)
        for c in range(tiles // 2):
            acc[at, c * 512 : (c + 1) * 512] += half[c * fb : (c + 1) * fb, :]

    for second in range(2):
        @pl.loop(0, places)
        def _(p):
            j = second * places + p

            @pl.when(valid[j] > 0)
            def _():
                fetch(j, p, second, lambda copy: copy.wait())
                add_block(j)

    expand = ones_where(iota((256, ab), 0) // 4 == iota((256, ab), 1))
    same_i = iota((256, 256), 0) % 4 == iota((256, 256), 1) % 4
    whole = metric[...]
    high = whole.astype(BF)
    low = (whole - high.astype(F32)).astype(BF)

    def widen(part):
        tall = nt_dot(expand, part).astype(BF)
        return jnp.where(same_i, nt_dot(tall, expand), 0.0).astype(BF)

    metric_high = widen(high)
    metric_low = widen(low)
    lane_from = iota((256, 256), 0)
    lane_to = iota((256, 256), 1)
    order = ones_where(
        ((lane_from // 4) % 4) * 64 + (lane_from // 16) * 4 + lane_from % 4 == lane_to
    )

    @pl.loop(0, nbasis // (SUBS * rb))
    def _(step):
        for sub in range(SUBS):
            xs, ys, zs = xs_all[sub], ys_all[sub], zs_all[sub]
            place = step * SUBS + sub
            at = pl.ds(pl.multiple_of(place * rb, rb), rb)
            for v in range(4):
                for ch in range(2):
                    parts = [
                        acc[at, (4 * ch + j) * 512 + v * 128 : (4 * ch + j) * 512 + v * 128 + 128]
                        for j in range(4)
                    ]
                    parts = swap_groups(parts)
                    for g in range(4):
                        xs[(4 * v + g) * rb : (4 * v + g + 1) * rb, ch * 128 : ch * 128 + 128] = parts[g]
            x = xs[...]
            x_high = x.astype(BF)
            x_low = (x - x_high.astype(F32)).astype(BF)
            y = nn_dot(x_high, metric_high) + nn_dot(x_low, metric_high) + nn_dot(x_high, metric_low)
            ys[...] = y.astype(BF).astype(YT)
            for ch in range(2):
                for h in range(2):
                    parts = [
                        ys[(8 * ch + j) * rb : (8 * ch + j + 1) * rb, h * 128 : h * 128 + 128]
                        for j in range(8)
                    ]
                    parts = swap_groups(parts)
                    for g in range(8):
                        zs[(8 * h + g) * rb : (8 * h + g + 1) * rb, ch * 128 : ch * 128 + 128] = parts[g].astype(BF)
            f = nn_dot(zs[...], order).astype(BF)
            for c in range(tiles):
                fitted[at, c * 256 : (c + 1) * 256] = f[c * rb : (c + 1) * rb, :]
            pltpu.make_async_copy(fitted.at[at, :], fitted_out.at[at, :], out_sem.at[place]).start()

    total[...] = jnp.zeros((nbasis, nbasis), F32)

    @pl.loop(0, wide // 1024)
    def _(k):
        part = fitted[:, pl.ds(pl.multiple_of(k * 1024, 1024), 1024)]
        total[...] += nt_dot(part, part)

    pick = ones_where(row_of[...] == iota((nbasis, nbasis), 1))
    partial_out[...] = nn_dot(pick, total[...].astype(BF)).astype(BF)

    @pl.loop(0, nbasis // rb)
    def _(step):
        at = pl.ds(pl.multiple_of(step * rb, rb), rb)
        pltpu.make_async_copy(fitted.at[at, :], fitted_out.at[at, :], out_sem.at[step]).wait()


def owner(kind, valid, mu_of, nu_of, order_of, row, blocks, panel, metric, row_of, plane_rows, fb):
    rows = valid.shape[0]
    nbasis, occ = panel.shape
    ab = metric.shape[0]
    rb = 32
    wide = ab * occ
    vmem = pl.BlockSpec(memory_space=pltpu.VMEM)
    anywhere = pl.BlockSpec(memory_space=pl.ANY)
    sizes = (rows, nbasis, fb, ab, occ, rb, plane_rows)
    return pl.pallas_call(
        functools.partial(owner_kernel, kind, len(blocks), sizes),
        out_shape=(
            jax.ShapeDtypeStruct((nbasis, wide), BF),
            jax.ShapeDtypeStruct((nbasis, nbasis), BF),
        ),
        grid_spec=pltpu.PrefetchScalarGridSpec(
            num_scalar_prefetch=5,
            grid=(1,),
            in_specs=[anywhere] * len(blocks) + [vmem, vmem, vmem],
            out_specs=(anywhere, vmem),
            scratch_shapes=[
                pltpu.VMEM((rows, fb, ab * fb), BF),
                pltpu.VMEM((nbasis, wide), F32),
                pltpu.VMEM((nbasis // fb, 8 * fb, 512), BF),
                [pltpu.VMEM((16 * rb, 256), F32)] * SUBS,
                [pltpu.VMEM((16 * rb, 256), YT)] * SUBS,
                [pltpu.VMEM((16 * rb, 256), BF)] * SUBS,
                pltpu.VMEM((nbasis, nbasis), F32),
                pltpu.VMEM((nbasis, wide), BF),
                pltpu.SemaphoreType.DMA((rows, 5)),
                pltpu.SemaphoreType.DMA((nbasis // rb,)),
            ],
        ),
        compiler_params=pltpu.CompilerParams(vmem_limit_bytes=60 << 20),
        name="owner",
    )(valid, mu_of, nu_of, order_of, row, *blocks, panel, metric, row_of)


PLANES = 8


def turn(x, count, by):
    return lax.ppermute(x, "pair", [(i, (i + by) % count) for i in range(count)])


def gather_panel(panel, count):
    rows = count // PLANES
    own = lax.axis_index("pair")
    whole = panel[None]
    while whole.shape[0] < rows:
        whole = jnp.concatenate([whole, turn(whole, count, PLANES * whole.shape[0])])
    whole = whole[lax.rem(own // PLANES - jnp.arange(rows) + rows, rows)][None]
    while whole.shape[0] < PLANES:
        by = whole.shape[0]
        pairs = [(i, (i // PLANES) * PLANES + (i % PLANES + by) % PLANES) for i in range(count)]
        whole = jnp.concatenate([whole, lax.ppermute(whole, "pair", pairs)])
    whole = whole[lax.rem(own % PLANES - jnp.arange(PLANES) + PLANES, PLANES)]
    return whole.transpose(1, 0, 2, 3).reshape(count * panel.shape[0], panel.shape[1])


def shards(three_center, panel, metric, screen, pair_blocks):
    pair_count = lax.axis_size("pair")
    column_count = lax.axis_size("aux")
    own = lax.axis_index("pair")
    rows = pair_count // PLANES
    slots, fb, inner = three_center.shape
    quarter = inner // 4
    ab = metric.shape[1]
    occ = panel.shape[1]
    nbasis = panel.shape[0] * pair_count

    targets = screen[:, :, 0]
    ids = jnp.arange(slots)
    earlier = ids[None, None, :] < ids[None, :, None]
    again = jnp.any((targets[:, :, None] == targets[:, None, :]) & earlier, axis=2)
    plane_of = targets % PLANES
    counts = jnp.sum(
        (again[:, :, None] & (plane_of[:, :, None] == jnp.arange(PLANES)[None, None, :])).astype(jnp.int32), axis=1
    )
    crowd = jnp.max(counts)
    own_targets = lax.dynamic_index_in_dim(targets, own, 0, keepdims=False)
    own_again = lax.dynamic_index_in_dim(again, own, 0, keepdims=False)
    own_planes = own_targets % PLANES
    own_order = jnp.sum(
        ((own_planes[:, None] == own_planes[None, :]) & own_again[None, :] & earlier[0]).astype(jnp.int32), axis=1
    )
    out_a, out_b, out_c, out_d = pack(
        crowd.reshape(1), own_targets, own_again.astype(jnp.int32), own_order, three_center, pair_count, PLANES
    )
    exchange = lambda x: lax.all_to_all(x, "pair", 0, 0, tiled=True)
    first = exchange(out_a)
    whole_panel = gather_panel(panel, pair_count)

    mine = targets == own
    hits = jnp.stack([mine & ~again, mine & again]).astype(jnp.int32)
    valid = jnp.sum(hits, axis=2).reshape(-1)
    mu_of = jnp.sum(hits * pair_blocks[None, :, :, 0], axis=2).reshape(-1)
    nu_of = jnp.sum(hits * pair_blocks[None, :, :, 1], axis=2).reshape(-1)
    here = again & (plane_of == own % PLANES)
    position = jnp.cumsum(here.astype(jnp.int32), axis=1) - here.astype(jnp.int32)
    order_of = jnp.sum(hits[1] * position, axis=1)

    share = nbasis // (pair_count * column_count)
    row_of = jnp.arange(nbasis).reshape(pair_count, column_count, share)
    row_of = row_of.transpose(1, 0, 2).reshape(nbasis, 1)
    row = (own // PLANES).reshape(1)

    def finish(kind, blocks):
        return owner(
            kind, valid, mu_of, nu_of, order_of, row, blocks, whole_panel, metric[0], row_of, rows, fb
        )

    def passed_round(lanes):
        left = turn(lanes, pair_count, PLANES)
        right = turn(lanes, pair_count, -PLANES)
        half = pair_count // 2
        return left, right, turn(left[:half], pair_count, PLANES), turn(right[half:], pair_count, -PLANES)

    def few():
        later = exchange(out_b)
        return finish(1, (first, later) + passed_round(first[:, :, 2 * quarter :]))

    def some():
        later = exchange(out_c)
        return finish(2, (first, later) + passed_round(first[:, :, quarter:]))

    def many():
        return finish(3, (first, exchange(out_b), exchange(out_d)))

    fitted, partial = lax.switch(jnp.clip(crowd - 1, 0, 2), (few, some, many))

    partial = lax.all_to_all(
        partial.reshape(column_count, nbasis // column_count, nbasis), "aux", 0, 0, tiled=True
    )
    partial = jnp.sum(partial.astype(F32), axis=0).reshape(pair_count, share, nbasis)
    partial = lax.all_to_all(partial, "pair", 0, 0, tiled=True)
    norm_factor = 1.0 / (pair_count * column_count * ab * occ)
    return (fitted[None], jnp.sum(partial, axis=0) * norm_factor)


def solution(mesh):
    return jax.shard_map(
        shards,
        mesh=mesh,
        in_specs=(
            P(("pair", "aux"), None, None),
            P("pair", None),
            P(("pair", "aux"), None, None),
            P(None, "aux", None),
            P(None, "aux", None),
        ),
        out_specs=(P(("pair", "aux"), None, None), P(("pair", "aux"), None)),
        check_vma=False,
    )
```

```python
import functools
import jax
import jax.numpy as jnp
from jax import lax
from jax.experimental import pallas as pl
from jax.experimental.pallas import tpu as pltpu
from jax.sharding import PartitionSpec as P

BF = jnp.bfloat16
F32 = jnp.float32
SUBS = 4
YT = jnp.float32


def iota(shape, dim):
    return lax.broadcasted_iota(jnp.int32, shape, dim)


def ones_where(mask):
    return jnp.where(mask, 1.0, 0.0).astype(BF)


def nt_dot(a, b):
    return lax.dot_general(a, b, (((1,), (1,)), ((), ())), preferred_element_type=F32)


def nn_dot(a, b):
    return jnp.dot(a, b, preferred_element_type=F32)


def pack_kernel(sizes, target, blocks, panel, out, held, flat, seen, in_sem, out_sem, panel_sem):
    slots, owners, capacity = sizes
    fb = held.shape[1]
    tiles = held.shape[2] // 128
    length = flat.shape[1]

    def fetch(s):
        return pltpu.make_async_copy(blocks.at[s], held.at[s], in_sem.at[s])

    def put(s, rank):
        at = pl.ds(pl.multiple_of(rank * length, length), length)
        return pltpu.make_async_copy(flat.at[s], out.at[target[s], at, :], out_sem.at[s])

    def put_panel(p):
        return pltpu.make_async_copy(
            panel, out.at[p, pl.ds(capacity * length, panel.shape[0]), :], panel_sem.at[p]
        )

    @pl.loop(0, slots)
    def _(s):
        fetch(s).start()

    @pl.loop(0, owners)
    def _(p):
        put_panel(p).start()
        seen[p] = 0

    @pl.loop(0, slots)
    def _(s):
        fetch(s).wait()
        for c in range(tiles):
            row = (c % 2) * (length // 2) + (c // 2) * fb
            flat[s, row : row + fb, :] = held[s, :, c * 128 : (c + 1) * 128]
        rank = seen[target[s]]
        seen[target[s]] = rank + 1
        put(s, rank).start()

    @pl.loop(0, slots)
    def _(s):
        put(s, 0).wait()

    @pl.loop(0, owners)
    def _(p):
        put_panel(p).wait()


def pack(target, blocks, panel, owners, capacity):
    slots, fb, inner = blocks.shape
    length = fb * inner // 128
    return pl.pallas_call(
        functools.partial(pack_kernel, (slots, owners, capacity)),
        out_shape=jax.ShapeDtypeStruct((owners, capacity * length + panel.shape[0], 128), blocks.dtype),
        grid_spec=pltpu.PrefetchScalarGridSpec(
            num_scalar_prefetch=1,
            grid=(1,),
            in_specs=[pl.BlockSpec(memory_space=pl.ANY), pl.BlockSpec(memory_space=pltpu.VMEM)],
            out_specs=pl.BlockSpec(memory_space=pl.ANY),
            scratch_shapes=[
                pltpu.VMEM((slots, fb, inner), blocks.dtype),
                pltpu.VMEM((slots, length, 128), blocks.dtype),
                pltpu.SMEM((owners,), jnp.int32),
                pltpu.SemaphoreType.DMA((slots,)),
                pltpu.SemaphoreType.DMA((slots,)),
                pltpu.SemaphoreType.DMA((owners,)),
            ],
        ),
        compiler_params=pltpu.CompilerParams(vmem_limit_bytes=60 << 20),
        name="pack",
    )(target, blocks, panel)


def swap_groups(parts):
    count = len(parts)
    group = 128 // count
    lane_group = iota(parts[0].shape, 1) // group
    step = count // 2
    while step:
        low = (lane_group & step) == 0
        done = list(parts)
        for j in range(count):
            if j & step:
                continue
            a, b = parts[j], parts[j + step]
            done[j] = jnp.where(low, a, pltpu.roll(b, group * step, 1))
            done[j + step] = jnp.where(low, pltpu.roll(a, 128 - group * step, 1), b)
        parts = done
        step //= 2
    return parts


def owner_kernel(
    sizes, valid, mu_of, nu_of, arrived, metric, row_of, fitted_out, partial_out,
    held, panel, acc, weights, xs_all, ys_all, zs_all, fitted, total, in_sem, out_sem, panel_sem,
):
    rows, nbasis, fb, ab, occ, rb, capacity = sizes
    length = held.shape[1]
    nblk = nbasis // fb
    tiles = ab // 4
    wide = ab * occ

    def fetch(j):
        at = pl.ds(pl.multiple_of(lax.rem(j, capacity) * length, length), length)
        return pltpu.make_async_copy(arrived.at[lax.div(j, capacity), at, :], held.at[j], in_sem.at[j])

    fetch_panel = pltpu.make_async_copy(
        arrived.at[:, pl.ds(capacity * length, panel.shape[1]), :], panel, panel_sem
    )
    fetch_panel.start()

    @pl.loop(0, rows)
    def _(j):
        @pl.when(valid[j] > 0)
        def _():
            fetch(j).start()

    @pl.loop(0, nbasis // 8)
    def _(r):
        acc[pl.ds(pl.multiple_of(r * 8, 8), 8), :] = jnp.zeros((8, wide), F32)

    pick_row = iota((8 * fb, fb // 2), 0) % fb // 2 == iota((8 * fb, fb // 2), 1)
    same_half = iota((8 * fb, 128), 0) % 2 == iota((8 * fb, 128), 1) // occ
    spread_row = iota((128, 512), 0) % occ
    spread_col = iota((128, 512), 1)
    spread = ones_where((spread_col // 32) * 4 + spread_col % 4 == spread_row)
    same_q = iota((8 * fb, 512), 0) // fb == (iota((8 * fb, 512), 1) // 4) % 8
    pick_row = ones_where(pick_row)
    per_block = fb // 2 // panel.shape[1]
    fetch_panel.wait()

    @pl.loop(0, nblk)
    def _(n):
        part = jnp.concatenate([panel[n * per_block + k].astype(F32) for k in range(per_block)], axis=0)
        tall = jnp.where(same_half, nn_dot(pick_row, part.astype(BF)), 0.0).astype(BF)
        weights[n] = jnp.where(same_q, nn_dot(tall, spread), 0.0).astype(BF)

    @pl.loop(0, rows)
    def _(j):
        @pl.when(valid[j] > 0)
        def _():
            fetch(j).wait()
            block = held[j]
            lhs = jnp.concatenate([block[: length // 2], block[length // 2 :]], axis=1)
            half = nn_dot(lhs, weights[nu_of[j]])
            at = pl.ds(pl.multiple_of(mu_of[j] * fb, fb), fb)
            for c in range(tiles // 2):
                acc[at, c * 512 : (c + 1) * 512] += half[c * fb : (c + 1) * fb, :]

    expand = ones_where(iota((256, ab), 0) // 4 == iota((256, ab), 1))
    same_i = iota((256, 256), 0) % 4 == iota((256, 256), 1) % 4
    whole = metric[...]
    high = whole.astype(BF)
    low = (whole - high.astype(F32)).astype(BF)

    def widen(part):
        tall = nt_dot(expand, part).astype(BF)
        return jnp.where(same_i, nt_dot(tall, expand), 0.0).astype(BF)

    metric_high = widen(high)
    metric_low = widen(low)
    lane_from = iota((256, 256), 0)
    lane_to = iota((256, 256), 1)
    order = ones_where(
        ((lane_from // 4) % 4) * 64 + (lane_from // 16) * 4 + lane_from % 4 == lane_to
    )

    @pl.loop(0, nbasis // (SUBS * rb))
    def _(step):
        for sub in range(SUBS):
            xs, ys, zs = xs_all[sub], ys_all[sub], zs_all[sub]
            place = step * SUBS + sub
            at = pl.ds(pl.multiple_of(place * rb, rb), rb)
            for v in range(4):
                for ch in range(2):
                    parts = [
                        acc[at, (4 * ch + j) * 512 + v * 128 : (4 * ch + j) * 512 + v * 128 + 128]
                        for j in range(4)
                    ]
                    parts = swap_groups(parts)
                    for g in range(4):
                        xs[(4 * v + g) * rb : (4 * v + g + 1) * rb, ch * 128 : ch * 128 + 128] = parts[g]
            x = xs[...]
            x_high = x.astype(BF)
            x_low = (x - x_high.astype(F32)).astype(BF)
            y = nn_dot(x_high, metric_high) + nn_dot(x_low, metric_high) + nn_dot(x_high, metric_low)
            ys[...] = y.astype(BF).astype(YT)
            for ch in range(2):
                for h in range(2):
                    parts = [
                        ys[(8 * ch + j) * rb : (8 * ch + j + 1) * rb, h * 128 : h * 128 + 128]
                        for j in range(8)
                    ]
                    parts = swap_groups(parts)
                    for g in range(8):
                        zs[(8 * h + g) * rb : (8 * h + g + 1) * rb, ch * 128 : ch * 128 + 128] = parts[g].astype(BF)
            f = nn_dot(zs[...], order).astype(BF)
            for c in range(tiles):
                fitted[at, c * 256 : (c + 1) * 256] = f[c * rb : (c + 1) * rb, :]
            pltpu.make_async_copy(fitted.at[at, :], fitted_out.at[at, :], out_sem.at[place]).start()

    total[...] = jnp.zeros((nbasis, nbasis), F32)

    @pl.loop(0, wide // 1024)
    def _(k):
        part = fitted[:, pl.ds(pl.multiple_of(k * 1024, 1024), 1024)]
        total[...] += nt_dot(part, part)

    pick = ones_where(row_of[...] == iota((nbasis, nbasis), 1))
    partial_out[...] = nn_dot(pick, total[...].astype(BF)).astype(BF)

    @pl.loop(0, nbasis // rb)
    def _(step):
        at = pl.ds(pl.multiple_of(step * rb, rb), rb)
        pltpu.make_async_copy(fitted.at[at, :], fitted_out.at[at, :], out_sem.at[step]).wait()


def owner(valid, mu_of, nu_of, arrived, metric, row_of, fb, occ):
    rows = valid.shape[0]
    owners = arrived.shape[0]
    capacity = rows // owners
    nbasis = row_of.shape[0]
    ab = metric.shape[0]
    length = fb * ab * fb // 128
    rb = 32
    wide = ab * occ
    vmem = pl.BlockSpec(memory_space=pltpu.VMEM)
    anywhere = pl.BlockSpec(memory_space=pl.ANY)
    return pl.pallas_call(
        functools.partial(owner_kernel, (rows, nbasis, fb, ab, occ, rb, capacity)),
        out_shape=(
            jax.ShapeDtypeStruct((nbasis, wide), BF),
            jax.ShapeDtypeStruct((nbasis, nbasis), BF),
        ),
        grid_spec=pltpu.PrefetchScalarGridSpec(
            num_scalar_prefetch=3,
            grid=(1,),
            in_specs=[anywhere, vmem, vmem],
            out_specs=(anywhere, vmem),
            scratch_shapes=[
                pltpu.VMEM((rows, length, 128), BF),
                pltpu.VMEM((owners, arrived.shape[1] - capacity * length, 128), BF),
                pltpu.VMEM((nbasis, wide), F32),
                pltpu.VMEM((nbasis // fb, 8 * fb, 512), BF),
                [pltpu.VMEM((16 * rb, 256), F32)] * SUBS,
                [pltpu.VMEM((16 * rb, 256), YT)] * SUBS,
                [pltpu.VMEM((16 * rb, 256), BF)] * SUBS,
                pltpu.VMEM((nbasis, wide), BF),
                pltpu.VMEM((nbasis, nbasis), F32),
                pltpu.SemaphoreType.DMA((rows,)),
                pltpu.SemaphoreType.DMA((nbasis // rb,)),
                pltpu.SemaphoreType.DMA,
            ],
        ),
        compiler_params=pltpu.CompilerParams(vmem_limit_bytes=60 << 20),
        name="owner",
    )(valid, mu_of, nu_of, arrived, metric, row_of)


def shards(three_center, panel, metric, screen, pair_blocks):
    pair_count = lax.axis_size("pair")
    column_count = lax.axis_size("aux")
    own = lax.axis_index("pair")
    slots, fb, inner = three_center.shape
    ab = metric.shape[1]
    occ = panel.shape[1]
    nbasis = panel.shape[0] * pair_count
    capacity = 2
    targets = screen[:, :, 0]
    own_targets = lax.dynamic_index_in_dim(targets, own, 0, keepdims=False)
    outgoing = pack(own_targets, three_center, panel.reshape(-1, 128), pair_count, capacity)
    arrived = lax.all_to_all(outgoing, "pair", 0, 0, tiled=True)

    mine = targets == own
    before = jnp.cumsum(mine.astype(jnp.int32), axis=1) - mine.astype(jnp.int32)
    hits = mine[:, None, :] & (before[:, None, :] == jnp.arange(capacity)[None, :, None])
    flat = pair_count * capacity
    valid = jnp.sum(hits.astype(jnp.int32), axis=2).reshape(flat)
    mu_of = jnp.sum(jnp.where(hits, pair_blocks[:, None, :, 0], 0), axis=2).reshape(flat)
    nu_of = jnp.sum(jnp.where(hits, pair_blocks[:, None, :, 1], 0), axis=2).reshape(flat)

    share = nbasis // (pair_count * column_count)
    row_of = jnp.arange(nbasis).reshape(pair_count, column_count, share)
    row_of = row_of.transpose(1, 0, 2).reshape(nbasis, 1)
    fitted, partial = owner(valid, mu_of, nu_of, arrived, metric[0], row_of, fb, occ)
    partial = lax.all_to_all(
        partial.reshape(column_count, nbasis // column_count, nbasis), "aux", 0, 0, tiled=True
    )
    partial = jnp.sum(partial.astype(F32), axis=0).reshape(pair_count, share, nbasis)
    partial = lax.all_to_all(partial, "pair", 0, 0, tiled=True)
    norm_factor = 1.0 / (pair_count * column_count * ab * occ)
    return (fitted[None], jnp.sum(partial, axis=0) * norm_factor)


def solution(mesh):
    return jax.shard_map(
        shards,
        mesh=mesh,
        in_specs=(
            P(("pair", "aux"), None, None),
            P("pair", None),
            P(("pair", "aux"), None, None),
            P(None, "aux", None),
            P(None, "aux", None),
        ),
        out_specs=(P(("pair", "aux"), None, None), P(("pair", "aux"), None)),
        check_vma=False,
    )
```

```python
import functools
import jax
import jax.numpy as jnp
from jax import lax
from jax.experimental import pallas as pl
from jax.experimental.pallas import tpu as pltpu
from jax.sharding import PartitionSpec as P

BF = jnp.bfloat16
F32 = jnp.float32
SUBS = 4
GROUP = 4
WSTEP = 4
YT = jnp.float32


def iota(shape, dim):
    return lax.broadcasted_iota(jnp.int32, shape, dim)


def ones_where(mask):
    return jnp.where(mask, 1.0, 0.0).astype(BF)


def nt_dot(a, b):
    return lax.dot_general(a, b, (((1,), (1,)), ((), ())), preferred_element_type=F32)


def nn_dot(a, b):
    return jnp.dot(a, b, preferred_element_type=F32)


def pack_kernel(sizes, target, blocks, panel, out, held, flat, seen, in_sem, out_sem, panel_sem):
    slots, owners, capacity = sizes
    fb = held.shape[1]
    tiles = held.shape[2] // 128
    length = flat.shape[1]

    def fetch(s):
        return pltpu.make_async_copy(blocks.at[s], held.at[s], in_sem.at[s])

    def put(s, rank):
        at = pl.ds(pl.multiple_of(rank * length, length), length)
        return pltpu.make_async_copy(flat.at[s], out.at[target[s], at, :], out_sem.at[s])

    def put_panel(p):
        return pltpu.make_async_copy(
            panel, out.at[p, pl.ds(capacity * length, panel.shape[0]), :], panel_sem.at[p]
        )

    @pl.loop(0, slots)
    def _(s):
        fetch(s).start()

    @pl.loop(0, owners)
    def _(p):
        put_panel(p).start()
        seen[p] = 0

    @pl.loop(0, slots)
    def _(s):
        fetch(s).wait()
        for c in range(tiles):
            row = (c % 2) * (length // 2) + (c // 2) * fb
            flat[s, row : row + fb, :] = held[s, :, c * 128 : (c + 1) * 128]
        rank = seen[target[s]]
        seen[target[s]] = rank + 1
        put(s, rank).start()

    @pl.loop(0, slots)
    def _(s):
        put(s, 0).wait()

    @pl.loop(0, owners)
    def _(p):
        put_panel(p).wait()


def pack(target, blocks, panel, owners, capacity):
    slots, fb, inner = blocks.shape
    length = fb * inner // 128
    return pl.pallas_call(
        functools.partial(pack_kernel, (slots, owners, capacity)),
        out_shape=jax.ShapeDtypeStruct((owners, capacity * length + panel.shape[0], 128), blocks.dtype),
        grid_spec=pltpu.PrefetchScalarGridSpec(
            num_scalar_prefetch=1,
            grid=(1,),
            in_specs=[pl.BlockSpec(memory_space=pl.ANY), pl.BlockSpec(memory_space=pltpu.VMEM)],
            out_specs=pl.BlockSpec(memory_space=pl.ANY),
            scratch_shapes=[
                pltpu.VMEM((slots, fb, inner), blocks.dtype),
                pltpu.VMEM((slots, length, 128), blocks.dtype),
                pltpu.SMEM((owners,), jnp.int32),
                pltpu.SemaphoreType.DMA((slots,)),
                pltpu.SemaphoreType.DMA((slots,)),
                pltpu.SemaphoreType.DMA((owners,)),
            ],
        ),
        compiler_params=pltpu.CompilerParams(vmem_limit_bytes=60 << 20),
        name="pack",
    )(target, blocks, panel)


def swap_groups(parts):
    count = len(parts)
    group = 128 // count
    lane_group = iota(parts[0].shape, 1) // group
    step = count // 2
    while step:
        low = (lane_group & step) == 0
        done = list(parts)
        for j in range(count):
            if j & step:
                continue
            a, b = parts[j], parts[j + step]
            done[j] = jnp.where(low, a, pltpu.roll(b, group * step, 1))
            done[j + step] = jnp.where(low, pltpu.roll(a, 128 - group * step, 1), b)
        parts = done
        step //= 2
    return parts


def owner_kernel(
    sizes, valid, mu_of, nu_of, arrived, metric, row_of, fitted_out, partial_out,
    held, panel, acc, weights, xs_all, ys_all, zs_all, fitted, total, listed, tally, in_sem, out_sem, panel_sem,
):
    rows, nbasis, fb, ab, occ, rb, capacity = sizes
    length = held.shape[1]
    nblk = nbasis // fb
    tiles = ab // 4
    wide = ab * occ

    def fetch(j):
        at = pl.ds(pl.multiple_of(lax.rem(j, capacity) * length, length), length)
        return pltpu.make_async_copy(arrived.at[lax.div(j, capacity), at, :], held.at[j], in_sem.at[j])

    fetch_panel = pltpu.make_async_copy(
        arrived.at[:, pl.ds(capacity * length, panel.shape[1]), :], panel, panel_sem
    )
    fetch_panel.start()

    tally[0] = 0

    @pl.loop(0, rows)
    def _(j):
        listed[j] = 0

    @pl.loop(0, rows)
    def _(j):
        @pl.when(valid[j] > 0)
        def _():
            fetch(j).start()
            listed[tally[0]] = j
            tally[0] = tally[0] + 1

    count = tally[0]

    @pl.loop(0, nbasis // 8)
    def _(r):
        acc[pl.ds(pl.multiple_of(r * 8, 8), 8), :] = jnp.zeros((8, wide), F32)

    pick_row = ones_where(iota((fb, fb // 2), 0) // 2 == iota((fb, fb // 2), 1))
    same_half = iota((fb, 128), 0) % 2 == iota((fb, 128), 1) // occ
    spread_row = iota((128, 512), 0) % occ
    spread_col = iota((128, 512), 1)
    spread = ones_where((spread_col // 32) * 4 + spread_col % 4 == spread_row)
    column_q = (iota((fb, 512), 1) // 4) % 8
    per_block = fb // 2 // panel.shape[1]
    fetch_panel.wait()

    @pl.loop(0, nblk // WSTEP)
    def _(step):
        for k in range(WSTEP):
            n = step * WSTEP + k
            part = jnp.concatenate([panel[n * per_block + k].astype(F32) for k in range(per_block)], axis=0)
            tall = jnp.where(same_half, nn_dot(pick_row, part.astype(BF)), 0.0).astype(BF)
            broad = nn_dot(tall, spread)
            for q in range(8):
                weights[n, q * fb : (q + 1) * fb, :] = jnp.where(column_q == q, broad, 0.0).astype(BF)

    held[rows] = jnp.zeros(held.shape[1:], BF)

    @pl.loop(0, (count + GROUP - 1) // GROUP)
    def _(step):
        picks = []
        for k in range(GROUP):
            at = step * GROUP + k
            there = at < count
            j = listed[jnp.minimum(at, rows - 1)]

            @pl.when(there)
            def _():
                fetch(j).wait()

            picks.append((jnp.where(there, j, rows), jnp.where(there, mu_of[j], 0), jnp.where(there, nu_of[j], 0)))
        halves = []
        for j, mu, nu in picks:
            block = held[j]
            lhs = jnp.concatenate([block[: length // 2], block[length // 2 :]], axis=1)
            halves.append(nn_dot(lhs, weights[nu]))
        for (j, mu, nu), half in zip(picks, halves):
            at = pl.ds(pl.multiple_of(mu * fb, fb), fb)
            for c in range(tiles // 2):
                acc[at, c * 512 : (c + 1) * 512] += half[c * fb : (c + 1) * fb, :]

    expand = ones_where(iota((256, ab), 0) // 4 == iota((256, ab), 1))
    same_i = iota((256, 256), 0) % 4 == iota((256, 256), 1) % 4
    whole = metric[...]
    high = whole.astype(BF)
    low = (whole - high.astype(F32)).astype(BF)

    def widen(part):
        tall = nt_dot(expand, part).astype(BF)
        return jnp.where(same_i, nt_dot(tall, expand), 0.0).astype(BF)

    metric_high = widen(high)
    metric_low = widen(low)
    metric_all = jnp.concatenate([metric_high, metric_high, metric_low], axis=0)
    lane_from = iota((256, 256), 0)
    lane_to = iota((256, 256), 1)
    order = ones_where(
        ((lane_from // 4) % 4) * 64 + (lane_from // 16) * 4 + lane_from % 4 == lane_to
    )

    @pl.loop(0, nbasis // (SUBS * rb))
    def _(step):
        for sub in range(SUBS):
            xs, ys, zs = xs_all[sub], ys_all[sub], zs_all[sub]
            place = step * SUBS + sub
            at = pl.ds(pl.multiple_of(place * rb, rb), rb)
            for v in range(4):
                for ch in range(2):
                    parts = [
                        acc[at, (4 * ch + j) * 512 + v * 128 : (4 * ch + j) * 512 + v * 128 + 128]
                        for j in range(4)
                    ]
                    parts = swap_groups(parts)
                    for g in range(4):
                        xs[(4 * v + g) * rb : (4 * v + g + 1) * rb, ch * 128 : ch * 128 + 128] = parts[g]
            x = xs[...]
            x_high = x.astype(BF)
            x_low = (x - x_high.astype(F32)).astype(BF)
            y = nn_dot(jnp.concatenate([x_high, x_low, x_high], axis=1), metric_all)
            ys[...] = y.astype(BF).astype(YT)
            for ch in range(2):
                for h in range(2):
                    parts = [
                        ys[(8 * ch + j) * rb : (8 * ch + j + 1) * rb, h * 128 : h * 128 + 128]
                        for j in range(8)
                    ]
                    parts = swap_groups(parts)
                    for g in range(8):
                        zs[(8 * h + g) * rb : (8 * h + g + 1) * rb, ch * 128 : ch * 128 + 128] = parts[g].astype(BF)
            f = nn_dot(zs[...], order).astype(BF)
            for c in range(tiles):
                fitted[at, c * 256 : (c + 1) * 256] = f[c * rb : (c + 1) * rb, :]
            pltpu.make_async_copy(fitted.at[at, :], fitted_out.at[at, :], out_sem.at[place]).start()

    total[...] = jnp.zeros((nbasis, nbasis), F32)

    @pl.loop(0, wide // 1024)
    def _(k):
        part = fitted[:, pl.ds(pl.multiple_of(k * 1024, 1024), 1024)]
        total[...] += nt_dot(part, part)

    pick = ones_where(row_of[...] == iota((nbasis, nbasis), 1))
    partial_out[...] = nn_dot(pick, total[...].astype(BF)).astype(BF)

    @pl.loop(0, nbasis // rb)
    def _(step):
        at = pl.ds(pl.multiple_of(step * rb, rb), rb)
        pltpu.make_async_copy(fitted.at[at, :], fitted_out.at[at, :], out_sem.at[step]).wait()


def owner(valid, mu_of, nu_of, arrived, metric, row_of, fb, occ):
    rows = valid.shape[0]
    owners = arrived.shape[0]
    capacity = rows // owners
    nbasis = row_of.shape[0]
    ab = metric.shape[0]
    length = fb * ab * fb // 128
    rb = 32
    wide = ab * occ
    vmem = pl.BlockSpec(memory_space=pltpu.VMEM)
    anywhere = pl.BlockSpec(memory_space=pl.ANY)
    return pl.pallas_call(
        functools.partial(owner_kernel, (rows, nbasis, fb, ab, occ, rb, capacity)),
        out_shape=(
            jax.ShapeDtypeStruct((nbasis, wide), BF),
            jax.ShapeDtypeStruct((nbasis, nbasis), BF),
        ),
        grid_spec=pltpu.PrefetchScalarGridSpec(
            num_scalar_prefetch=3,
            grid=(1,),
            in_specs=[anywhere, vmem, vmem],
            out_specs=(anywhere, vmem),
            scratch_shapes=[
                pltpu.VMEM((rows + 1, length, 128), BF),
                pltpu.VMEM((owners, arrived.shape[1] - capacity * length, 128), BF),
                pltpu.VMEM((nbasis, wide), F32),
                pltpu.VMEM((nbasis // fb, 8 * fb, 512), BF),
                [pltpu.VMEM((16 * rb, 256), F32)] * SUBS,
                [pltpu.VMEM((16 * rb, 256), YT)] * SUBS,
                [pltpu.VMEM((16 * rb, 256), BF)] * SUBS,
                pltpu.VMEM((nbasis, wide), BF),
                pltpu.VMEM((nbasis, nbasis), F32),
                pltpu.SMEM((rows,), jnp.int32),
                pltpu.SMEM((1,), jnp.int32),
                pltpu.SemaphoreType.DMA((rows,)),
                pltpu.SemaphoreType.DMA((nbasis // rb,)),
                pltpu.SemaphoreType.DMA,
            ],
        ),
        compiler_params=pltpu.CompilerParams(vmem_limit_bytes=60 << 20),
        name="owner",
    )(valid, mu_of, nu_of, arrived, metric, row_of)


def shards(three_center, panel, metric, screen, pair_blocks):
    pair_count = lax.axis_size("pair")
    column_count = lax.axis_size("aux")
    own = lax.axis_index("pair")
    slots, fb, inner = three_center.shape
    ab = metric.shape[1]
    occ = panel.shape[1]
    nbasis = panel.shape[0] * pair_count
    capacity = 2
    targets = screen[:, :, 0]
    own_targets = lax.dynamic_index_in_dim(targets, own, 0, keepdims=False)
    outgoing = pack(own_targets, three_center, panel.reshape(-1, 128), pair_count, capacity)
    arrived = lax.all_to_all(outgoing, "pair", 0, 0, tiled=True)

    mine = targets == own
    before = jnp.cumsum(mine.astype(jnp.int32), axis=1) - mine.astype(jnp.int32)
    hits = mine[:, None, :] & (before[:, None, :] == jnp.arange(capacity)[None, :, None])
    flat = pair_count * capacity
    valid = jnp.sum(hits.astype(jnp.int32), axis=2).reshape(flat)
    mu_of = jnp.sum(jnp.where(hits, pair_blocks[:, None, :, 0], 0), axis=2).reshape(flat)
    nu_of = jnp.sum(jnp.where(hits, pair_blocks[:, None, :, 1], 0), axis=2).reshape(flat)

    share = nbasis // (pair_count * column_count)
    row_of = jnp.arange(nbasis).reshape(pair_count, column_count, share)
    row_of = row_of.transpose(1, 0, 2).reshape(nbasis, 1)
    fitted, partial = owner(valid, mu_of, nu_of, arrived, metric[0], row_of, fb, occ)
    partial = lax.all_to_all(
        partial.reshape(column_count, nbasis // column_count, nbasis), "aux", 0, 0, tiled=True
    )
    partial = jnp.sum(partial.astype(F32), axis=0).reshape(pair_count, share, nbasis)
    partial = lax.all_to_all(partial, "pair", 0, 0, tiled=True)
    norm_factor = 1.0 / (pair_count * column_count * ab * occ)
    return (fitted[None], jnp.sum(partial, axis=0) * norm_factor)


def solution(mesh):
    return jax.shard_map(
        shards,
        mesh=mesh,
        in_specs=(
            P(("pair", "aux"), None, None),
            P("pair", None),
            P(("pair", "aux"), None, None),
            P(None, "aux", None),
            P(None, "aux", None),
        ),
        out_specs=(P(("pair", "aux"), None, None), P(("pair", "aux"), None)),
        check_vma=False,
    )
```

```python
import functools
import jax
import jax.numpy as jnp
from jax import lax
from jax.experimental import pallas as pl
from jax.experimental.pallas import tpu as pltpu
from jax.sharding import PartitionSpec as P

BF = jnp.bfloat16
F32 = jnp.float32
SUBS = 4
GROUP = 4
WSTEP = 4
YT = jnp.float32


def iota(shape, dim):
    return lax.broadcasted_iota(jnp.int32, shape, dim)


def ones_where(mask):
    return jnp.where(mask, 1.0, 0.0).astype(BF)


def nt_dot(a, b):
    return lax.dot_general(a, b, (((1,), (1,)), ((), ())), preferred_element_type=F32)


def nn_dot(a, b):
    return jnp.dot(a, b, preferred_element_type=F32)


def pack_kernel(sizes, target, blocks, panel, out, held, flat, seen, in_sem, out_sem, panel_sem):
    slots, owners, capacity = sizes
    fb = held.shape[1]
    tiles = held.shape[2] // 128
    length = flat.shape[1]

    def fetch(s):
        return pltpu.make_async_copy(blocks.at[s], held.at[s], in_sem.at[s])

    def put(s, rank):
        at = pl.ds(pl.multiple_of(rank * length, length), length)
        return pltpu.make_async_copy(flat.at[s], out.at[target[s], at, :], out_sem.at[s])

    def put_panel(p):
        return pltpu.make_async_copy(
            panel, out.at[p, pl.ds(capacity * length, panel.shape[0]), :], panel_sem.at[p]
        )

    @pl.loop(0, slots)
    def _(s):
        fetch(s).start()

    @pl.loop(0, owners)
    def _(p):
        put_panel(p).start()
        seen[p] = 0

    @pl.loop(0, slots)
    def _(s):
        fetch(s).wait()
        for c in range(tiles):
            row = (c % 2) * (length // 2) + (c // 2) * fb
            flat[s, row : row + fb, :] = held[s, :, c * 128 : (c + 1) * 128]
        rank = seen[target[s]]
        seen[target[s]] = rank + 1
        put(s, rank).start()

    @pl.loop(0, slots)
    def _(s):
        put(s, 0).wait()

    @pl.loop(0, owners)
    def _(p):
        put_panel(p).wait()


def pack(target, blocks, panel, owners, capacity):
    slots, fb, inner = blocks.shape
    length = fb * inner // 128
    return pl.pallas_call(
        functools.partial(pack_kernel, (slots, owners, capacity)),
        out_shape=jax.ShapeDtypeStruct((owners, capacity * length + panel.shape[0], 128), blocks.dtype),
        grid_spec=pltpu.PrefetchScalarGridSpec(
            num_scalar_prefetch=1,
            grid=(1,),
            in_specs=[pl.BlockSpec(memory_space=pl.ANY), pl.BlockSpec(memory_space=pltpu.VMEM)],
            out_specs=pl.BlockSpec(memory_space=pl.ANY),
            scratch_shapes=[
                pltpu.VMEM((slots, fb, inner), blocks.dtype),
                pltpu.VMEM((slots, length, 128), blocks.dtype),
                pltpu.SMEM((owners,), jnp.int32),
                pltpu.SemaphoreType.DMA((slots,)),
                pltpu.SemaphoreType.DMA((slots,)),
                pltpu.SemaphoreType.DMA((owners,)),
            ],
        ),
        compiler_params=pltpu.CompilerParams(vmem_limit_bytes=60 << 20),
        name="pack",
    )(target, blocks, panel)


def swap_groups(parts):
    count = len(parts)
    group = 128 // count
    lane_group = iota(parts[0].shape, 1) // group
    step = count // 2
    while step:
        low = (lane_group & step) == 0
        done = list(parts)
        for j in range(count):
            if j & step:
                continue
            a, b = parts[j], parts[j + step]
            done[j] = jnp.where(low, a, pltpu.roll(b, group * step, 1))
            done[j + step] = jnp.where(low, pltpu.roll(a, 128 - group * step, 1), b)
        parts = done
        step //= 2
    return parts


def owner_kernel(
    sizes, number, arrived, metric, fitted_out, partial_out,
    held, panel, acc, weights, xs_all, ys_all, zs_all, fitted, total, listed, tally, in_sem, out_sem, panel_sem,
):
    rows, nbasis, fb, ab, occ, rb, capacity, columns, share = sizes
    length = held.shape[1]
    nblk = nbasis // fb
    tiles = ab // 4
    wide = ab * occ

    def fetch(j):
        at = pl.ds(pl.multiple_of(lax.rem(j, capacity) * length, length), length)
        return pltpu.make_async_copy(arrived.at[lax.div(j, capacity), at, :], held.at[j], in_sem.at[j])

    fetch_panel = pltpu.make_async_copy(
        arrived.at[:, pl.ds(capacity * length, panel.shape[1]), :], panel, panel_sem
    )
    fetch_panel.start()

    tally[0] = 0

    @pl.loop(0, rows)
    def _(j):
        listed[j] = 0

    @pl.loop(0, rows)
    def _(j):
        @pl.when(number[j] > 0)
        def _():
            fetch(j).start()
            listed[tally[0]] = j
            tally[0] = tally[0] + 1

    count = tally[0]

    @pl.loop(0, nbasis // 8)
    def _(r):
        acc[pl.ds(pl.multiple_of(r * 8, 8), 8), :] = jnp.zeros((8, wide), F32)

    pick_row = ones_where(iota((fb, fb // 2), 0) // 2 == iota((fb, fb // 2), 1))
    same_half = iota((fb, 128), 0) % 2 == iota((fb, 128), 1) // occ
    spread_row = iota((128, 512), 0) % occ
    spread_col = iota((128, 512), 1)
    spread = ones_where((spread_col // 32) * 4 + spread_col % 4 == spread_row)
    column_q = (iota((fb, 512), 1) // 4) % 8
    per_block = fb // 2 // panel.shape[1]
    fetch_panel.wait()

    @pl.loop(0, nblk // WSTEP)
    def _(step):
        for k in range(WSTEP):
            n = step * WSTEP + k
            part = jnp.concatenate([panel[n * per_block + k].astype(F32) for k in range(per_block)], axis=0)
            tall = jnp.where(same_half, nn_dot(pick_row, part.astype(BF)), 0.0).astype(BF)
            broad = nn_dot(tall, spread)
            for q in range(8):
                weights[n, q * fb : (q + 1) * fb, :] = jnp.where(column_q == q, broad, 0.0).astype(BF)

    held[rows] = jnp.zeros(held.shape[1:], BF)

    @pl.loop(0, (count + GROUP - 1) // GROUP)
    def _(step):
        picks = []
        for k in range(GROUP):
            at = step * GROUP + k
            there = at < count
            j = listed[jnp.minimum(at, rows - 1)]

            @pl.when(there)
            def _():
                fetch(j).wait()

            pair = jnp.where(there, number[j] - 1, 0)
            picks.append((jnp.where(there, j, rows), lax.div(pair, nblk), lax.rem(pair, nblk)))
        halves = []
        for j, mu, nu in picks:
            block = held[j]
            lhs = jnp.concatenate([block[: length // 2], block[length // 2 :]], axis=1)
            halves.append(nn_dot(lhs, weights[nu]))
        for (j, mu, nu), half in zip(picks, halves):
            at = pl.ds(pl.multiple_of(mu * fb, fb), fb)
            for c in range(tiles // 2):
                acc[at, c * 512 : (c + 1) * 512] += half[c * fb : (c + 1) * fb, :]

    expand = ones_where(iota((256, ab), 0) // 4 == iota((256, ab), 1))
    same_i = iota((256, 256), 0) % 4 == iota((256, 256), 1) % 4
    whole = metric[...]
    high = whole.astype(BF)
    low = (whole - high.astype(F32)).astype(BF)

    def widen(part):
        tall = nt_dot(expand, part).astype(BF)
        return jnp.where(same_i, nt_dot(tall, expand), 0.0).astype(BF)

    metric_high = widen(high)
    metric_low = widen(low)
    metric_all = jnp.concatenate([metric_high, metric_high, metric_low], axis=0)
    lane_from = iota((256, 256), 0)
    lane_to = iota((256, 256), 1)
    order = ones_where(
        ((lane_from // 4) % 4) * 64 + (lane_from // 16) * 4 + lane_from % 4 == lane_to
    )

    @pl.loop(0, nbasis // (SUBS * rb))
    def _(step):
        for sub in range(SUBS):
            xs, ys, zs = xs_all[sub], ys_all[sub], zs_all[sub]
            place = step * SUBS + sub
            at = pl.ds(pl.multiple_of(place * rb, rb), rb)
            for v in range(4):
                for ch in range(2):
                    parts = [
                        acc[at, (4 * ch + j) * 512 + v * 128 : (4 * ch + j) * 512 + v * 128 + 128]
                        for j in range(4)
                    ]
                    parts = swap_groups(parts)
                    for g in range(4):
                        xs[(4 * v + g) * rb : (4 * v + g + 1) * rb, ch * 128 : ch * 128 + 128] = parts[g]
            x = xs[...]
            x_high = x.astype(BF)
            x_low = (x - x_high.astype(F32)).astype(BF)
            y = nn_dot(jnp.concatenate([x_high, x_low, x_high], axis=1), metric_all)
            ys[...] = y.astype(BF).astype(YT)
            for ch in range(2):
                for h in range(2):
                    parts = [
                        ys[(8 * ch + j) * rb : (8 * ch + j + 1) * rb, h * 128 : h * 128 + 128]
                        for j in range(8)
                    ]
                    parts = swap_groups(parts)
                    for g in range(8):
                        zs[(8 * h + g) * rb : (8 * h + g + 1) * rb, ch * 128 : ch * 128 + 128] = parts[g].astype(BF)
            f = nn_dot(zs[...], order).astype(BF)
            for c in range(tiles):
                fitted[at, c * 256 : (c + 1) * 256] = f[c * rb : (c + 1) * rb, :]
            pltpu.make_async_copy(fitted.at[at, :], fitted_out.at[at, :], out_sem.at[place]).start()

    total[...] = jnp.zeros((nbasis, nbasis), F32)

    @pl.loop(0, wide // 1024)
    def _(k):
        part = fitted[:, pl.ds(pl.multiple_of(k * 1024, 1024), 1024)]
        total[...] += nt_dot(part, part)

    order_row = iota((nbasis, nbasis), 0)
    column, pair, e = order_row // (nbasis // columns), order_row // share % (nbasis // columns // share), order_row % share
    pick = ones_where((pair * columns + column) * share + e == iota((nbasis, nbasis), 1))
    partial_out[...] = nn_dot(pick, total[...].astype(BF)).astype(BF)

    @pl.loop(0, nbasis // rb)
    def _(step):
        at = pl.ds(pl.multiple_of(step * rb, rb), rb)
        pltpu.make_async_copy(fitted.at[at, :], fitted_out.at[at, :], out_sem.at[step]).wait()


def owner(number, arrived, metric, nbasis, columns, share, fb, occ):
    rows = number.shape[0]
    owners = arrived.shape[0]
    capacity = rows // owners
    ab = metric.shape[0]
    length = fb * ab * fb // 128
    rb = 32
    wide = ab * occ
    vmem = pl.BlockSpec(memory_space=pltpu.VMEM)
    anywhere = pl.BlockSpec(memory_space=pl.ANY)
    return pl.pallas_call(
        functools.partial(owner_kernel, (rows, nbasis, fb, ab, occ, rb, capacity, columns, share)),
        out_shape=(
            jax.ShapeDtypeStruct((nbasis, wide), BF),
            jax.ShapeDtypeStruct((nbasis, nbasis), BF),
        ),
        grid_spec=pltpu.PrefetchScalarGridSpec(
            num_scalar_prefetch=1,
            grid=(1,),
            in_specs=[anywhere, vmem],
            out_specs=(anywhere, vmem),
            scratch_shapes=[
                pltpu.VMEM((rows + 1, length, 128), BF),
                pltpu.VMEM((owners, arrived.shape[1] - capacity * length, 128), BF),
                pltpu.VMEM((nbasis, wide), F32),
                pltpu.VMEM((nbasis // fb, 8 * fb, 512), BF),
                [pltpu.VMEM((16 * rb, 256), F32)] * SUBS,
                [pltpu.VMEM((16 * rb, 256), YT)] * SUBS,
                [pltpu.VMEM((16 * rb, 256), BF)] * SUBS,
                pltpu.VMEM((nbasis, wide), BF),
                pltpu.VMEM((nbasis, nbasis), F32),
                pltpu.SMEM((rows,), jnp.int32),
                pltpu.SMEM((1,), jnp.int32),
                pltpu.SemaphoreType.DMA((rows,)),
                pltpu.SemaphoreType.DMA((nbasis // rb,)),
                pltpu.SemaphoreType.DMA,
            ],
        ),
        compiler_params=pltpu.CompilerParams(vmem_limit_bytes=60 << 20),
        name="owner",
    )(number, arrived, metric)


def shards(three_center, panel, metric, screen, pair_blocks):
    pair_count = lax.axis_size("pair")
    column_count = lax.axis_size("aux")
    own = lax.axis_index("pair")
    slots, fb, inner = three_center.shape
    ab = metric.shape[1]
    occ = panel.shape[1]
    nbasis = panel.shape[0] * pair_count
    capacity = 2
    targets = screen[:, :, 0]
    own_targets = lax.dynamic_index_in_dim(targets, own, 0, keepdims=False)
    mine = targets == own
    before = jnp.cumsum(mine.astype(jnp.int32), axis=1) - mine.astype(jnp.int32)
    hits = mine[:, None, :] & (before[:, None, :] == jnp.arange(capacity)[None, :, None])
    flat = pair_count * capacity
    blocks = nbasis // fb
    number = pair_blocks[:, None, :, 0] * blocks + pair_blocks[:, None, :, 1] + 1
    listed = jnp.sum(jnp.where(hits, number, 0), axis=2).reshape(flat)

    share = nbasis // (pair_count * column_count)
    own_targets, listed = lax.optimization_barrier((own_targets, listed))
    outgoing = pack(own_targets, three_center, panel.reshape(-1, 128), pair_count, capacity)
    arrived = lax.all_to_all(outgoing, "pair", 0, 0, tiled=True)

    fitted, partial = owner(
        listed, arrived, metric[0], nbasis, column_count, share, fb, occ
    )
    partial = lax.all_to_all(
        partial.reshape(column_count, nbasis // column_count, nbasis), "aux", 0, 0, tiled=True
    )
    partial = jnp.sum(partial.astype(F32), axis=0).reshape(pair_count, share, nbasis)
    partial = lax.all_to_all(partial, "pair", 0, 0, tiled=True)
    norm_factor = 1.0 / (pair_count * column_count * ab * occ)
    return (fitted[None], jnp.sum(partial, axis=0) * norm_factor)


def solution(mesh):
    return jax.shard_map(
        shards,
        mesh=mesh,
        in_specs=(
            P(("pair", "aux"), None, None),
            P("pair", None),
            P(("pair", "aux"), None, None),
            P(None, "aux", None),
            P(None, "aux", None),
        ),
        out_specs=(P(("pair", "aux"), None, None), P(("pair", "aux"), None)),
        check_vma=False,
    )
```

```python
import functools
import jax
import jax.numpy as jnp
from jax import lax
from jax.experimental import pallas as pl
from jax.experimental.pallas import tpu as pltpu
from jax.sharding import PartitionSpec as P

BF = jnp.bfloat16
F32 = jnp.float32
SUBS = 4
GROUP = 8
WSTEP = 4
YT = jnp.float32


def iota(shape, dim):
    return lax.broadcasted_iota(jnp.int32, shape, dim)


def ones_where(mask):
    return jnp.where(mask, 1.0, 0.0).astype(BF)


def nt_dot(a, b):
    return lax.dot_general(a, b, (((1,), (1,)), ((), ())), preferred_element_type=F32)


def nn_dot(a, b):
    return jnp.dot(a, b, preferred_element_type=F32)


def pack_kernel(sizes, target, blocks, rows, out, held, flat, panel, seen, in_sem, out_sem, panel_sem):
    slots, owners, capacity = sizes
    fb = held.shape[1]
    tiles = held.shape[2] // 128
    length = flat.shape[1]

    def fetch(s):
        return pltpu.make_async_copy(blocks.at[s], held.at[s], in_sem.at[s])

    def put(s, rank):
        at = pl.ds(pl.multiple_of(rank * length, length), length)
        return pltpu.make_async_copy(flat.at[s], out.at[target[s], at, :], out_sem.at[s])

    def put_panel(p):
        return pltpu.make_async_copy(
            panel, out.at[p, pl.ds(capacity * length, panel.shape[0]), :], panel_sem.at[p]
        )

    @pl.loop(0, slots)
    def _(s):
        fetch(s).start()

    lines = rows[...].astype(F32)
    half = panel.shape[0]
    panel[...] = jnp.concatenate([lines[:half], lines[half:]], axis=1).astype(panel.dtype)

    @pl.loop(0, owners)
    def _(p):
        put_panel(p).start()
        seen[p] = 0

    @pl.loop(0, slots)
    def _(s):
        fetch(s).wait()
        for c in range(tiles):
            row = (c % 2) * (length // 2) + (c // 2) * fb
            flat[s, row : row + fb, :] = held[s, :, c * 128 : (c + 1) * 128]
        rank = seen[target[s]]
        seen[target[s]] = rank + 1
        put(s, rank).start()

    @pl.loop(0, slots)
    def _(s):
        put(s, 0).wait()

    @pl.loop(0, owners)
    def _(p):
        put_panel(p).wait()


def pack(target, blocks, panel, owners, capacity):
    slots, fb, inner = blocks.shape
    length = fb * inner // 128
    return pl.pallas_call(
        functools.partial(pack_kernel, (slots, owners, capacity)),
        out_shape=jax.ShapeDtypeStruct((owners, capacity * length + panel.shape[0] // 2, 128), blocks.dtype),
        grid_spec=pltpu.PrefetchScalarGridSpec(
            num_scalar_prefetch=1,
            grid=(1,),
            in_specs=[pl.BlockSpec(memory_space=pl.ANY), pl.BlockSpec(memory_space=pltpu.VMEM)],
            out_specs=pl.BlockSpec(memory_space=pl.ANY),
            scratch_shapes=[
                pltpu.VMEM((slots, fb, inner), blocks.dtype),
                pltpu.VMEM((slots, length, 128), blocks.dtype),
                pltpu.VMEM((panel.shape[0] // 2, 128), blocks.dtype),
                pltpu.SMEM((owners,), jnp.int32),
                pltpu.SemaphoreType.DMA((slots,)),
                pltpu.SemaphoreType.DMA((slots,)),
                pltpu.SemaphoreType.DMA((owners,)),
            ],
        ),
        compiler_params=pltpu.CompilerParams(vmem_limit_bytes=60 << 20),
        name="pack",
    )(target, blocks, panel)


def swap_groups(parts):
    count = len(parts)
    group = 128 // count
    lane_group = iota(parts[0].shape, 1) // group
    step = count // 2
    while step:
        low = (lane_group & step) == 0
        done = list(parts)
        for j in range(count):
            if j & step:
                continue
            a, b = parts[j], parts[j + step]
            done[j] = jnp.where(low, a, pltpu.roll(b, group * step, 1))
            done[j + step] = jnp.where(low, pltpu.roll(a, 128 - group * step, 1), b)
        parts = done
        step //= 2
    return parts


def owner_kernel(
    sizes, number, arrived, metric, fitted_out, partial_out,
    held, panel, acc, weights, xs_all, ys_all, zs_all, fitted, total, listed, tally, in_sem, out_sem, panel_sem,
):
    rows, nbasis, fb, ab, occ, rb, capacity, columns, share = sizes
    length = held.shape[1]
    nblk = nbasis // fb
    tiles = ab // 4
    wide = ab * occ

    def fetch(j):
        at = pl.ds(pl.multiple_of(lax.rem(j, capacity) * length, length), length)
        return pltpu.make_async_copy(arrived.at[lax.div(j, capacity), at, :], held.at[j], in_sem.at[j])

    fetch_panel = pltpu.make_async_copy(
        arrived.at[:, pl.ds(capacity * length, panel.shape[1]), :], panel, panel_sem
    )
    fetch_panel.start()

    tally[0] = 0

    @pl.loop(0, rows)
    def _(j):
        listed[j] = 0

    @pl.loop(0, rows)
    def _(j):
        @pl.when(number[j] > 0)
        def _():
            fetch(j).start()
            listed[tally[0]] = j
            tally[0] = tally[0] + 1

    count = tally[0]

    @pl.loop(0, nbasis // 8)
    def _(r):
        acc[pl.ds(pl.multiple_of(r * 8, 8), 8), :] = jnp.zeros((8, wide), F32)

    near = panel.shape[1]
    row = iota((fb, fb // 2), 0)
    pick_row = ones_where(row // (2 * near) * near + row % near == iota((fb, fb // 2), 1))
    same_half = iota((fb, 128), 0) % (2 * near) // near == iota((fb, 128), 1) // occ
    spread_row = iota((128, 512), 0) % occ
    spread_col = iota((128, 512), 1)
    spread = ones_where((spread_col // 32) * 4 + spread_col % 4 == spread_row)
    column_q = (iota((fb, 512), 1) // 4) % 8
    per_block = fb // 2 // panel.shape[1]
    fetch_panel.wait()

    @pl.loop(0, nblk // WSTEP)
    def _(step):
        for k in range(WSTEP):
            n = step * WSTEP + k
            part = jnp.concatenate([panel[n * per_block + k].astype(F32) for k in range(per_block)], axis=0)
            tall = jnp.where(same_half, nn_dot(pick_row, part.astype(BF)), 0.0).astype(BF)
            broad = nn_dot(tall, spread)
            for q in range(8):
                weights[n, q * fb : (q + 1) * fb, :] = jnp.where(column_q == q, broad, 0.0).astype(BF)

    held[rows] = jnp.zeros(held.shape[1:], BF)

    @pl.loop(0, (count + GROUP - 1) // GROUP)
    def _(step):
        picks = []
        for k in range(GROUP):
            at = step * GROUP + k
            there = at < count
            j = listed[jnp.minimum(at, rows - 1)]

            @pl.when(there)
            def _():
                fetch(j).wait()

            pair = jnp.where(there, number[j] - 1, 0)
            picks.append((jnp.where(there, j, rows), lax.div(pair, nblk), lax.rem(pair, nblk)))
        halves = []
        for j, mu, nu in picks:
            block = held[j]
            lhs = jnp.concatenate([block[: length // 2], block[length // 2 :]], axis=1)
            halves.append(nn_dot(lhs, weights[nu]))
        for (j, mu, nu), half in zip(picks, halves):
            at = pl.ds(pl.multiple_of(mu * fb, fb), fb)
            for c in range(tiles // 2):
                acc[at, c * 512 : (c + 1) * 512] += half[c * fb : (c + 1) * fb, :]

    expand = ones_where(iota((256, ab), 0) // 4 == iota((256, ab), 1))
    same_i = iota((256, 256), 0) % 4 == iota((256, 256), 1) % 4
    whole = metric[...]
    high = whole.astype(BF)
    low = (whole - high.astype(F32)).astype(BF)

    def widen(part):
        tall = nt_dot(expand, part).astype(BF)
        return jnp.where(same_i, nt_dot(tall, expand), 0.0).astype(BF)

    metric_high = widen(high)
    metric_low = widen(low)
    metric_all = jnp.concatenate([metric_high, metric_high, metric_low], axis=0)
    lane_from = iota((256, 256), 0)
    lane_to = iota((256, 256), 1)
    order = ones_where(
        ((lane_from // 4) % 4) * 64 + (lane_from // 16) * 4 + lane_from % 4 == lane_to
    )

    @pl.loop(0, nbasis // (SUBS * rb))
    def _(step):
        for sub in range(SUBS):
            xs, ys, zs = xs_all[sub], ys_all[sub], zs_all[sub]
            place = step * SUBS + sub
            at = pl.ds(pl.multiple_of(place * rb, rb), rb)
            for v in range(4):
                for ch in range(2):
                    parts = [
                        acc[at, (4 * ch + j) * 512 + v * 128 : (4 * ch + j) * 512 + v * 128 + 128]
                        for j in range(4)
                    ]
                    parts = swap_groups(parts)
                    for g in range(4):
                        xs[(4 * v + g) * rb : (4 * v + g + 1) * rb, ch * 128 : ch * 128 + 128] = parts[g]
            x = xs[...]
            x_high = x.astype(BF)
            x_low = (x - x_high.astype(F32)).astype(BF)
            y = nn_dot(jnp.concatenate([x_high, x_low, x_high], axis=1), metric_all)
            ys[...] = y.astype(BF).astype(YT)
            for ch in range(2):
                for h in range(2):
                    parts = [
                        ys[(8 * ch + j) * rb : (8 * ch + j + 1) * rb, h * 128 : h * 128 + 128]
                        for j in range(8)
                    ]
                    parts = swap_groups(parts)
                    for g in range(8):
                        zs[(8 * h + g) * rb : (8 * h + g + 1) * rb, ch * 128 : ch * 128 + 128] = parts[g].astype(BF)
            f = nn_dot(zs[...], order).astype(BF)
            for c in range(tiles):
                fitted[at, c * 256 : (c + 1) * 256] = f[c * rb : (c + 1) * rb, :]
            pltpu.make_async_copy(fitted.at[at, :], fitted_out.at[at, :], out_sem.at[place]).start()

    total[...] = jnp.zeros((nbasis, nbasis), F32)

    @pl.loop(0, wide // 1024)
    def _(k):
        part = fitted[:, pl.ds(pl.multiple_of(k * 1024, 1024), 1024)]
        total[...] += nt_dot(part, part)

    order_row = iota((nbasis, nbasis), 0)
    column, pair, e = order_row // (nbasis // columns), order_row // share % (nbasis // columns // share), order_row % share
    pick = ones_where((pair * columns + column) * share + e == iota((nbasis, nbasis), 1))
    partial_out[...] = nn_dot(pick, total[...].astype(BF)).astype(BF)

    @pl.loop(0, nbasis // rb)
    def _(step):
        at = pl.ds(pl.multiple_of(step * rb, rb), rb)
        pltpu.make_async_copy(fitted.at[at, :], fitted_out.at[at, :], out_sem.at[step]).wait()


def owner(number, arrived, metric, nbasis, columns, share, fb, occ):
    rows = number.shape[0]
    owners = arrived.shape[0]
    capacity = rows // owners
    ab = metric.shape[0]
    length = fb * ab * fb // 128
    rb = 32
    wide = ab * occ
    vmem = pl.BlockSpec(memory_space=pltpu.VMEM)
    anywhere = pl.BlockSpec(memory_space=pl.ANY)
    return pl.pallas_call(
        functools.partial(owner_kernel, (rows, nbasis, fb, ab, occ, rb, capacity, columns, share)),
        out_shape=(
            jax.ShapeDtypeStruct((nbasis, wide), BF),
            jax.ShapeDtypeStruct((nbasis, nbasis), BF),
        ),
        grid_spec=pltpu.PrefetchScalarGridSpec(
            num_scalar_prefetch=1,
            grid=(1,),
            in_specs=[anywhere, vmem],
            out_specs=(anywhere, vmem),
            scratch_shapes=[
                pltpu.VMEM((rows + 1, length, 128), BF),
                pltpu.VMEM((owners, arrived.shape[1] - capacity * length, 128), BF),
                pltpu.VMEM((nbasis, wide), F32),
                pltpu.VMEM((nbasis // fb, 8 * fb, 512), BF),
                [pltpu.VMEM((16 * rb, 256), F32)] * SUBS,
                [pltpu.VMEM((16 * rb, 256), YT)] * SUBS,
                [pltpu.VMEM((16 * rb, 256), BF)] * SUBS,
                pltpu.VMEM((nbasis, wide), BF),
                pltpu.VMEM((nbasis, nbasis), F32),
                pltpu.SMEM((rows,), jnp.int32),
                pltpu.SMEM((1,), jnp.int32),
                pltpu.SemaphoreType.DMA((rows,)),
                pltpu.SemaphoreType.DMA((nbasis // rb,)),
                pltpu.SemaphoreType.DMA,
            ],
        ),
        compiler_params=pltpu.CompilerParams(vmem_limit_bytes=60 << 20),
        name="owner",
    )(number, arrived, metric)


def shards(three_center, panel, metric, screen, pair_blocks):
    pair_count = lax.axis_size("pair")
    column_count = lax.axis_size("aux")
    own = lax.axis_index("pair")
    slots, fb, inner = three_center.shape
    ab = metric.shape[1]
    occ = panel.shape[1]
    nbasis = panel.shape[0] * pair_count
    capacity = 2
    targets = screen[:, :, 0]
    own_targets = lax.dynamic_index_in_dim(targets, own, 0, keepdims=False)
    mine = targets == own
    before = jnp.cumsum(mine.astype(jnp.int32), axis=1) - mine.astype(jnp.int32)
    hits = mine[:, None, :] & (before[:, None, :] == jnp.arange(capacity)[None, :, None])
    flat = pair_count * capacity
    blocks = nbasis // fb
    number = pair_blocks[:, None, :, 0] * blocks + pair_blocks[:, None, :, 1] + 1
    listed = jnp.sum(jnp.where(hits, number, 0), axis=2).reshape(flat)

    share = nbasis // (pair_count * column_count)
    own_targets, listed = lax.optimization_barrier((own_targets, listed))
    outgoing = pack(own_targets, three_center, panel, pair_count, capacity)
    arrived = lax.all_to_all(outgoing, "pair", 0, 0, tiled=True)

    fitted, partial = owner(
        listed, arrived, metric[0], nbasis, column_count, share, fb, occ
    )
    partial = lax.all_to_all(
        partial.reshape(column_count, nbasis // column_count, nbasis), "aux", 0, 0, tiled=True
    )
    partial = jnp.sum(partial.astype(F32), axis=0).reshape(pair_count, share, nbasis)
    partial = lax.all_to_all(partial, "pair", 0, 0, tiled=True)
    norm_factor = 1.0 / (pair_count * column_count * ab * occ)
    return (fitted[None], jnp.sum(partial, axis=0) * norm_factor)


def solution(mesh):
    return jax.shard_map(
        shards,
        mesh=mesh,
        in_specs=(
            P(("pair", "aux"), None, None),
            P("pair", None),
            P(("pair", "aux"), None, None),
            P(None, "aux", None),
            P(None, "aux", None),
        ),
        out_specs=(P(("pair", "aux"), None, None), P(("pair", "aux"), None)),
        check_vma=False,
    )
```
